32 devices in a mesh: col: 16 (over z, x, core), tok: 2 (over y).
Axes of the slice: x: 2, y: 2, z: 4, core: 2. Of those that a mesh axis runs over, the one named last changes fastest.
Arguments:
- acts: bfloat16 [512, 8192], P('tok', 'col'), may hold values from -6 to 6
- grad_out: bfloat16 [512, 8192], P('tok', 'col'), may hold values from -0.19921875 to 0.19921875
- left_factor: float32 [8, 8192, 1024], P('tok', 'col'), may hold values from -6 to 6
- right_factor: float32 [8, 8192, 1024], P('tok', 'col'), may hold values from -6 to 6
- left_basis: bfloat16 [8, 8192, 1024], P('tok', 'col'), may hold values from -0.1875 to 0.1875
- right_basis: bfloat16 [8, 8192, 1024], P('tok', 'col'), may hold values from -0.1875 to 0.1875
- moment: float32 [8192, 8192], P('tok', 'col'), may hold values from -2 to 2
- second: float32 [8192, 8192], P('tok', 'col'), may hold values from 0.05 to 2
Outputs:
- left_out: float32 [8, 8192, 1024], P('tok', 'col')
- right_out: float32 [8, 8192, 1024], P('tok', 'col')
- moment_out: float32 [8192, 8192], P('tok', 'col')
- second_out: float32 [8192, 8192], P('tok', 'col')
- update: bfloat16 [8192, 8192], P('tok', 'col')
The draws below stay inside these ranges and needn't reach their ends.
All inputs are finite; a program needn't handle non-finite values.
Results may differ from the reference program's by a relative error of at most 0.0075.
Values may be sent and summed in bfloat16 or wider, within the bound.
No kernel may reach another device: no remote copies, remote signals or barrier semaphores. Data moves between devices by JAX's collectives and lax.ppermute only.
A program may use at most 192 MiB of HBM per device.

```python
import math
import jax
import jax.numpy as jnp
from jax import lax

D = 8192
B = 1024
TOKENS = 512


def steps_of(own_key, shape, pieces, least, largest):
    def one(dim, shards_of):
        draws = jax.random.uniform(jax.random.fold_in(jax.random.fold_in(own_key, 6), dim), (shards_of,), jnp.float32, least / len(pieces), largest / len(pieces))
        return jnp.repeat(jnp.exp(draws), shape[dim] // shards_of).reshape((-1,) + (1,) * (len(shape) - dim - 1))

    gain = one(*pieces[0])
    for cut in pieces[1:]:
        gain = gain * one(*cut)
    return gain


def scatter_about(rng, dims, scale, reach, pieces=(), held_as=jnp.bfloat16):
    array = jax.random.normal(rng, dims, jnp.float32) * scale
    if len(pieces) > 0:
        array = steps_of(rng, dims, pieces, -0.22, 0.18) * array
    return jnp.clip(array, min=-reach, max=reach).astype(held_as)


def setup_inputs(seed: int = 0) -> dict:
    seeds = jax.random.split(jax.random.key(seed), 9)
    acts = scatter_about(seeds[0], (TOKENS, D), 1.0, 6.0, ((0, 2), (1, 16)))
    grad_out = scatter_about(seeds[1], (TOKENS, D), 0.03, 0.19921875, ((0, 2), (1, 16)))
    left_factor = scatter_about(seeds[2], (D // B, D, B), 1.0, 6.0, ((0, 2), (1, 16)), jnp.float32)
    right_factor = scatter_about(seeds[3], (D // B, D, B), 1.0, 6.0, ((0, 2), (1, 16)), jnp.float32)
    left_basis = scatter_about(seeds[4], (D // B, D, B), B ** -0.5, 0.1875, ((0, 2), (1, 16)))
    right_basis = scatter_about(seeds[5], (D // B, D, B), B ** -0.5, 0.1875, ((0, 2), (1, 16)))
    moment = scatter_about(seeds[6], (D, D), 0.3, 2.0, ((0, 2), (1, 16)), jnp.float32)
    second = jnp.clip(jnp.exp(math.log(2.0) - 3.6888794 * jax.random.uniform(seeds[7], (D, D), jnp.float32) ** steps_of(seeds[7], (D, D), ((0, 2), (1, 16)), -0.2, 0.2)), 0.05, 2.0)
    return dict(acts=acts, grad_out=grad_out, left_factor=left_factor, right_factor=right_factor, left_basis=left_basis, right_basis=right_basis, moment=moment, second=second)


shampoo_beta = 0.95
first_beta = 0.9
second_beta = 0.95
first_corr = 1.0 - 0.9 ** 4
second_corr = 1.0 - 0.95 ** 4
epsilon = 1e-08

def one_block(pack):
    grads, left_fac, right_fac, left_q, right_q, first_m, second_m = pack
    left_new = shampoo_beta * left_fac + (1.0 - shampoo_beta) * jnp.dot(grads, grads.T, preferred_element_type=jnp.float32)
    right_new = shampoo_beta * right_fac + (1.0 - shampoo_beta) * jnp.dot(grads.T, grads, preferred_element_type=jnp.float32)
    mixed = jnp.dot(grads, right_q, preferred_element_type=jnp.float32).astype(jnp.bfloat16)
    rotated = jnp.dot(left_q.T, mixed, preferred_element_type=jnp.float32)
    first_new = first_beta * first_m + (1.0 - first_beta) * rotated
    second_new = second_beta * second_m + (1.0 - second_beta) * rotated * rotated
    normed = (first_new / first_corr / (jnp.sqrt(second_new / second_corr) + epsilon)).astype(jnp.bfloat16)
    back = jnp.dot(normed, right_q.T, preferred_element_type=jnp.float32).astype(jnp.bfloat16)
    update = jnp.dot(left_q, back, preferred_element_type=jnp.float32).astype(jnp.bfloat16)
    return (left_new, right_new, first_new, second_new, update)

def reference(acts, grad_out, left_factor, right_factor, left_basis, right_basis, moment, second):
    count = D // B
    grad = lax.dot_general(acts, grad_out, (((0,), (0,)), ((), ())), preferred_element_type=jnp.float32)
    tiles = grad.astype(jnp.bfloat16)

    def blockify(whole):
        return whole.reshape(count, B, count, B).transpose(0, 2, 1, 3).reshape(count * count, B, B)

    def unblock(blocked):
        return blocked.reshape(count, count, B, B).transpose(0, 2, 1, 3).reshape(D, D)

    def factored(whole):
        return whole.reshape(count * count, B, B)
    results = lax.map(one_block, (blockify(tiles), factored(left_factor), factored(right_factor), factored(left_basis), factored(right_basis), blockify(moment), blockify(second)))
    left_out = results[0].reshape(count, D, B)
    right_out = results[1].reshape(count, D, B)
    return (left_out, right_out, unblock(results[2]), unblock(results[3]), unblock(results[4]))
```

```python
import functools

import jax
import jax.numpy as jnp
from jax import lax
from jax.experimental import pallas as pl
from jax.experimental.pallas import tpu as pltpu
from jax.sharding import PartitionSpec as P

B = 1024


shampoo_beta = 0.95
first_beta = 0.9
second_beta = 0.95
first_corr = 1.0 - 0.9**4
second_corr = 1.0 - 0.95**4
epsilon = 1e-08

f32 = jnp.float32
bf16 = jnp.bfloat16


def dot(a, b, ca, cb):
    return lax.dot_general(a, b, (((ca,), (cb,)), ((), ())), preferred_element_type=f32)


def swapped(array, axis, distance):
    return lax.ppermute(array, axis, [(i, i ^ 1 << distance) for i in range(lax.axis_size(axis))])


def join_pair(current, incoming, axis, lower):
    width = current.shape[axis]
    shape = list(current.shape)
    shape[axis] = 2 * width
    joined = jnp.zeros(shape, current.dtype)
    mine_at = jnp.where(lower, 0, width)
    theirs_at = width - mine_at
    joined = lax.dynamic_update_slice_in_dim(joined, current, mine_at, axis)
    return lax.dynamic_update_slice_in_dim(joined, incoming, theirs_at, axis)


def normalized(first_new, second_new):
    return (first_new / first_corr / (jnp.sqrt(second_new / second_corr) + epsilon)).astype(bf16)


def general(acts, grad_out, left_factor, right_factor, left_basis, right_basis, moment, second):
    width = grad_out.shape[1]
    blocks = left_factor.shape[0]
    groups = B // width
    nbits = groups.bit_length() - 1
    member = lax.axis_index("col") % groups
    contract = (((0,), (0,)), ((), ()))
    whole = lax.all_gather(acts, "col", axis=1, tiled=True)
    block_rows = lax.all_to_all(whole, "tok", split_axis=1, concat_axis=0, tiled=True)
    all_grads = lax.all_gather(grad_out, "tok", axis=0, tiled=True)
    grad = lax.dot_general(block_rows, all_grads, contract, preferred_element_type=f32)
    own = grad.astype(bf16).reshape(blocks, B, width)
    tiles, left_full, right_full = (own, left_basis, right_basis)
    for bit in range(nbits):
        other = swapped((tiles, left_full, right_full), "col", bit)
        lower = member >> bit & 1 == 0
        tiles = join_pair(tiles, other[0], 2, lower)
        left_full = join_pair(left_full, other[1], 1, lower)
        right_full = join_pair(right_full, other[2], 1, lower)
    right_cols = lax.dynamic_slice_in_dim(right_full, member * width, width, 2)
    mixed = jnp.einsum("nab,nbc->nac", tiles, right_cols, preferred_element_type=f32).astype(bf16)
    lead = lax.dynamic_slice_in_dim(tiles, member * width, width, 1)
    left_new = shampoo_beta * left_factor + (1.0 - shampoo_beta) * jnp.einsum(
        "nab,ncb->nac", lead, tiles, preferred_element_type=f32
    )
    right_new = shampoo_beta * right_factor + (1.0 - shampoo_beta) * jnp.einsum(
        "nat,nab->ntb", own, tiles, preferred_element_type=f32
    )
    rotated = jnp.einsum("nab,nac->nbc", left_full, mixed, preferred_element_type=f32)
    first_new = first_beta * moment.reshape(blocks, B, width) + (1.0 - first_beta) * rotated
    second_new = (
        second_beta * second.reshape(blocks, B, width) + (1.0 - second_beta) * rotated * rotated
    )
    steps_full = normalized(first_new, second_new)
    for bit in range(nbits):
        other_steps = swapped(steps_full, "col", bit)
        lower = member >> bit & 1 == 0
        steps_full = join_pair(steps_full, other_steps, 2, lower)
    back = jnp.einsum("nab,ncb->nac", steps_full, right_basis, preferred_element_type=f32).astype(bf16)
    update = jnp.einsum("nab,nbc->nac", left_full, back, preferred_element_type=f32).astype(bf16)
    rows = blocks * B
    return (
        left_new,
        right_new,
        first_new.reshape(rows, width),
        second_new.reshape(rows, width),
        update.reshape(rows, width),
    )


def early_kernel(half_ref, g0_ref, g1_ref, h0_ref, h1_ref, right_own_ref, right_other_ref, x_ref, full_ref, gram_ref):
    tokens, width = g0_ref.shape
    at = pl.ds(pl.multiple_of(half_ref[0] * width, width), width)
    away = pl.ds(pl.multiple_of((1 - half_ref[0]) * width, width), width)

    @pl.when(pl.program_id(0) == 0)
    def _():
        full_ref[:tokens, at] = g0_ref[...]
        full_ref[tokens:, at] = g1_ref[...]
        full_ref[:tokens, away] = h0_ref[...]
        full_ref[tokens:, away] = h1_ref[...]
        gram_ref[...] = dot(full_ref[...], full_ref[...], 1, 1).astype(bf16)

    x = dot(full_ref[:, at], right_own_ref[0], 1, 0) + dot(full_ref[:, away], right_other_ref[0], 1, 0)
    x_ref[0] = x.astype(bf16)


def early(half, grads, right_own, right_other):
    blocks, width, order = right_own.shape
    tokens = 2 * grads[0].shape[0]
    whole = lambda n, s: (0, 0)
    column = pl.BlockSpec((1, width, width), lambda n, s: (n, 0, s[0]))
    return pl.pallas_call(
        early_kernel,
        grid_spec=pltpu.PrefetchScalarGridSpec(
            num_scalar_prefetch=1,
            grid=(blocks,),
            in_specs=[pl.BlockSpec((tokens // 2, width), whole)] * 4 + [column, column],
            out_specs=[
                pl.BlockSpec((1, tokens, width), lambda n, s: (n, 0, 0)),
                pl.BlockSpec((tokens, order), whole),
                pl.BlockSpec((tokens, tokens), whole),
            ],
        ),
        out_shape=[
            jax.ShapeDtypeStruct((blocks, tokens, width), bf16),
            jax.ShapeDtypeStruct((tokens, order), bf16),
            jax.ShapeDtypeStruct((tokens, tokens), bf16),
        ],
        compiler_params=pltpu.CompilerParams(vmem_limit_bytes=60 << 20),
        cost_estimate=pl.CostEstimate(
            flops=2 * blocks * tokens * order * width + 2 * tokens * tokens * order,
            bytes_accessed=2 * blocks * width * (order + tokens) + 4 * tokens * order,
            transcendentals=0,
        ),
        name="early",
    )(half, *grads, right_own, right_other)


def step_kernel(count, scal_ref, *refs):
    quads = refs[: 4 * count]
    (full_ref, gram_ref, x_ref, ql_own_ref, ql_other_ref, lf_ref, rf_ref, mo_ref, se_ref) = refs[
        4 * count : 4 * count + 9
    ]
    lo_ref, ro_ref, mout_ref, sout_ref, norm_ref, acts, left, right, mixed = refs[-9:]
    n, s = pl.program_id(0), pl.program_id(1)
    tokens, width = quads[0].shape
    half = scal_ref[0]
    at = pl.ds(pl.multiple_of(half * width, width), width)
    away = pl.ds(pl.multiple_of((1 - half) * width, width), width)

    for m in range(count):

        @pl.when((s == 0) & (n == m))
        def _():
            acts[:tokens, at] = quads[4 * m][...]
            acts[tokens:, at] = quads[4 * m + 1][...]
            acts[:tokens, away] = quads[4 * m + 2][...]
            acts[tokens:, away] = quads[4 * m + 3][...]

    @pl.when(s == 0)
    def _():
        a = acts[...]
        mixed[...] = dot(a, x_ref[0], 0, 0).astype(bf16)
        gram = dot(a, a, 1, 1).astype(bf16)
        left[...] = dot(acts[:, at], gram_ref[...], 0, 0).astype(bf16)
        right[...] = dot(full_ref[:, at], gram, 0, 0).astype(bf16)

    piece = mout_ref.shape[1]
    part = pl.ds(pl.multiple_of(s * piece, piece), piece)
    rot = dot(ql_own_ref[0], mixed[at, :], 0, 0) + dot(ql_other_ref[0], mixed[away, :], 0, 0)
    first_new = first_beta * mo_ref[0] + (1.0 - first_beta) * rot
    second_new = second_beta * se_ref[0] + (1.0 - second_beta) * rot * rot
    mout_ref[0] = first_new
    sout_ref[0] = second_new
    norm_ref[0] = normalized(first_new, second_new)
    lo_ref[0] = shampoo_beta * lf_ref[0] + (1.0 - shampoo_beta) * dot(left[...], acts[:, part], 1, 0)
    ro_ref[0] = shampoo_beta * rf_ref[0] + (1.0 - shampoo_beta) * dot(right[...], full_ref[:, part], 1, 0)


def step_blocks(scal, quads, shared, per_block, carried, pieces=2):
    count = len(quads)
    full, gram, x = shared
    lf, rf, mo, se = per_block[2:]
    tokens, order = full.shape
    blocks, width, _ = lf.shape
    piece = order // pieces
    factor = pl.BlockSpec((1, width, piece), lambda n, s, c: (c[1 + n], 0, s))
    moment = pl.BlockSpec((1, piece, width), lambda n, s, c: (c[1 + n], s, 0))
    once = lambda shape: pl.BlockSpec(shape, lambda n, s, c: (0, 0), pipeline_mode=pl.Buffered(1))
    in_specs = [once((tokens // 2, width))] * (4 * count) + [once((tokens, order)), once((tokens, tokens))]
    in_specs += [pl.BlockSpec((1, tokens, width), lambda n, s, c: (c[1 + n], 0, 0))]
    in_specs += [factor, factor, factor, factor, moment, moment]
    in_specs += [pl.BlockSpec(memory_space=pl.ANY)] * len(carried)
    first_carried = 1 + 4 * count + 9

    def kernel(*refs):
        at = first_carried
        step_kernel(count, *refs[:at], *refs[at + len(carried) :])

    shapes = [(lf.shape, f32), (rf.shape, f32), (mo.shape, f32), (se.shape, f32), ((count, order, width), bf16)]
    unit = 2 * tokens * tokens * width
    return pl.pallas_call(
        kernel,
        grid_spec=pltpu.PrefetchScalarGridSpec(
            num_scalar_prefetch=1,
            grid=(count, pieces),
            in_specs=in_specs,
            out_specs=[factor, factor, moment, moment, pl.BlockSpec((1, piece, width), lambda n, s, c: (n, s, 0))],
            scratch_shapes=[
                pltpu.VMEM((tokens, order), bf16),
                pltpu.VMEM((width, tokens), bf16),
                pltpu.VMEM((width, tokens), bf16),
                pltpu.VMEM((order, width), bf16),
            ],
        ),
        out_shape=[jax.ShapeDtypeStruct(*a) for a in shapes],
        input_output_aliases={first_carried + i: i for i in range(len(carried))},
        compiler_params=pltpu.CompilerParams(vmem_limit_bytes=60 << 20),
        cost_estimate=pl.CostEstimate(
            flops=14 * count * unit,
            bytes_accessed=count * 18 * order * width,
            transcendentals=2 * count * order * width,
        ),
        name="step",
    )(scal, *[a for q in quads for a in q], full, gram, x, *per_block, *carried)


def update_kernel(carried, scal_ref, n_own_ref, n_other_ref, q_own_ref, q_other_ref, ql_own_ref, ql_other_ref, *rest):
    out_ref, back = rest[carried:]
    width = q_own_ref.shape[1]
    half = scal_ref[0]
    b = dot(n_own_ref[0], q_own_ref[0], 1, 1) + dot(n_other_ref[0], q_other_ref[0], 1, 1)
    back[...] = b.astype(bf16)
    at = pl.ds(pl.multiple_of(half * width, width), width)
    away = pl.ds(pl.multiple_of((1 - half) * width, width), width)
    out_ref[0, at, :] = dot(ql_own_ref[0], back[...], 1, 0).astype(bf16)
    out_ref[0, away, :] = dot(ql_other_ref[0], back[...], 1, 0).astype(bf16)


def update_blocks(scal, norm_own, norm_other, right_own, ql_own, ql_other, carried):
    count, order, width = norm_own.shape
    blocks = ql_own.shape[0]
    stepped = pl.BlockSpec((1, order, width), lambda n, c: (n, 0, 0))
    basis = pl.BlockSpec((1, width, order), lambda n, c: (c[1 + n], 0, 0))
    unit = 2 * width * width * width
    return pl.pallas_call(
        functools.partial(update_kernel, len(carried)),
        grid_spec=pltpu.PrefetchScalarGridSpec(
            num_scalar_prefetch=1,
            grid=(count,),
            in_specs=[
                stepped,
                stepped,
                pl.BlockSpec((1, width, width), lambda n, c: (c[1 + n], 0, c[0])),
                pl.BlockSpec((1, width, width), lambda n, c: (c[1 + n], 0, 1 - c[0])),
                basis,
                basis,
            ]
            + [pl.BlockSpec(memory_space=pl.ANY)] * len(carried),
            out_specs=pl.BlockSpec((1, order, width), lambda n, c: (c[1 + n], 0, 0)),
            scratch_shapes=[pltpu.VMEM((order, width), bf16)],
        ),
        out_shape=jax.ShapeDtypeStruct((blocks, order, width), bf16),
        input_output_aliases={7: 0} if carried else {},
        compiler_params=pltpu.CompilerParams(vmem_limit_bytes=60 << 20),
        cost_estimate=pl.CostEstimate(
            flops=8 * count * unit, bytes_accessed=count * 8 * order * width, transcendentals=0
        ),
        name="update",
    )(scal, norm_own, norm_other, right_own, right_own, ql_own, ql_other, *carried)


def cube(acts, grad_out, left_factor, right_factor, left_basis, right_basis, moment, second):
    tokens, width = grad_out.shape
    blocks = left_factor.shape[0]
    size = lax.axis_size("col")
    col, y = lax.axis_index("col"), lax.axis_index("tok")
    half = col & 1
    high = col >> (size.bit_length() - 2) & 1
    first_block = (col >> 1 & (blocks - 1)) ^ jnp.where(high == y, 0, 2)

    def hop(array, mask):
        return lax.ppermute(array, "col", [(i, i ^ mask) for i in range(size)])

    def across(array):
        return lax.ppermute(array, "tok", [(0, 1), (1, 0)])

    core = lambda array: hop(array, 1)
    x_hop = lambda array: hop(array, 2)
    a_hop = lambda array: hop(array, 4)
    inner = high == y
    mirrored = hop(acts, size - 4)
    grads_away = across(grad_out)
    ql_other = core(left_basis)
    q_other = core(right_basis)
    grads = (grad_out, grads_away, core(grad_out), core(grads_away))
    near = jnp.where(inner, acts, mirrored)
    far = across(jnp.where(inner, mirrored, acts))
    near_x, near_a = x_hop(near), a_hop(near)
    far_x, far_a = x_hop(far), a_hop(far)
    near_d, far_d = x_hop(near_a), a_hop(far_x)
    quad = lambda n, f: (n, f, core(n), core(f))
    quad0, quad_x, quad_a, quad_d = quad(near, far), quad(near_x, far_x), quad(near_a, far_a), quad(near_d, far_d)

    as_scal = lambda *v: jnp.stack([jnp.asarray(a, jnp.int32) for a in v])
    x, full, gram = early(as_scal(half), grads, right_basis, q_other)
    shared = (full, gram, x)
    shaped = (blocks, B, width)
    states = [left_factor, right_factor, moment.reshape(shaped), second.reshape(shaped)]
    per_block = (left_basis, ql_other, *states)
    s0 = as_scal(half, first_block)
    s1 = as_scal(half, first_block ^ 1, first_block ^ 2)
    s2 = as_scal(half, first_block ^ 3)
    *outs, norm0 = step_blocks(s0, [quad0], shared, per_block, [])
    *outs, norm1 = step_blocks(s1, [quad_x, quad_a], shared, per_block, outs)
    *outs, norm2 = step_blocks(s2, [quad_d], shared, per_block, outs)
    update = update_blocks(s0, norm0, core(norm0), right_basis, left_basis, ql_other, [])
    update = update_blocks(s1, norm1, core(norm1), right_basis, left_basis, ql_other, [update])
    update = update_blocks(s2, norm2, core(norm2), right_basis, left_basis, ql_other, [update])
    rows = blocks * B
    left_new, right_new, first_new, second_new = outs
    return (
        left_new,
        right_new,
        first_new.reshape(rows, width),
        second_new.reshape(rows, width),
        update.reshape(rows, width),
    )


def shards(acts, grad_out, *rest):
    blocks = rest[0].shape[0]
    pairs = B // grad_out.shape[1] == 2 and lax.axis_size("tok") == 2
    if pairs and blocks == 4 and lax.axis_size("col") == 4 * blocks:
        return cube(acts, grad_out, *rest)
    return general(acts, grad_out, *rest)


def solution(mesh):
    in_specs = (
        P("tok", "col"),
        P("tok", "col"),
        P("tok", "col", None),
        P("tok", "col", None),
        P("tok", "col", None),
        P("tok", "col", None),
        P("tok", "col"),
        P("tok", "col"),
    )
    out_specs = (
        P("tok", "col", None),
        P("tok", "col", None),
        P("tok", "col"),
        P("tok", "col"),
        P("tok", "col"),
    )
    return jax.shard_map(shards, mesh=mesh, in_specs=in_specs, out_specs=out_specs, check_vma=False)
```

```python
import functools

import jax
import jax.numpy as jnp
from jax import lax
from jax.experimental import pallas as pl
from jax.experimental.pallas import tpu as pltpu
from jax.sharding import PartitionSpec as P

B = 1024


shampoo_beta = 0.95
first_beta = 0.9
second_beta = 0.95
first_corr = 1.0 - 0.9**4
second_corr = 1.0 - 0.95**4
epsilon = 1e-08

f32 = jnp.float32
bf16 = jnp.bfloat16


def dot(a, b, ca, cb):
    return lax.dot_general(a, b, (((ca,), (cb,)), ((), ())), preferred_element_type=f32)


def swapped(array, axis, distance):
    return lax.ppermute(array, axis, [(i, i ^ 1 << distance) for i in range(lax.axis_size(axis))])


def join_pair(current, incoming, axis, lower):
    width = current.shape[axis]
    shape = list(current.shape)
    shape[axis] = 2 * width
    joined = jnp.zeros(shape, current.dtype)
    mine_at = jnp.where(lower, 0, width)
    theirs_at = width - mine_at
    joined = lax.dynamic_update_slice_in_dim(joined, current, mine_at, axis)
    return lax.dynamic_update_slice_in_dim(joined, incoming, theirs_at, axis)


def normalized(first_new, second_new):
    return (first_new / first_corr / (jnp.sqrt(second_new / second_corr) + epsilon)).astype(bf16)


def general(acts, grad_out, left_factor, right_factor, left_basis, right_basis, moment, second):
    width = grad_out.shape[1]
    blocks = left_factor.shape[0]
    groups = B // width
    nbits = groups.bit_length() - 1
    member = lax.axis_index("col") % groups
    contract = (((0,), (0,)), ((), ()))
    whole = lax.all_gather(acts, "col", axis=1, tiled=True)
    block_rows = lax.all_to_all(whole, "tok", split_axis=1, concat_axis=0, tiled=True)
    all_grads = lax.all_gather(grad_out, "tok", axis=0, tiled=True)
    grad = lax.dot_general(block_rows, all_grads, contract, preferred_element_type=f32)
    own = grad.astype(bf16).reshape(blocks, B, width)
    tiles, left_full, right_full = (own, left_basis, right_basis)
    for bit in range(nbits):
        other = swapped((tiles, left_full, right_full), "col", bit)
        lower = member >> bit & 1 == 0
        tiles = join_pair(tiles, other[0], 2, lower)
        left_full = join_pair(left_full, other[1], 1, lower)
        right_full = join_pair(right_full, other[2], 1, lower)
    right_cols = lax.dynamic_slice_in_dim(right_full, member * width, width, 2)
    mixed = jnp.einsum("nab,nbc->nac", tiles, right_cols, preferred_element_type=f32).astype(bf16)
    lead = lax.dynamic_slice_in_dim(tiles, member * width, width, 1)
    left_new = shampoo_beta * left_factor + (1.0 - shampoo_beta) * jnp.einsum(
        "nab,ncb->nac", lead, tiles, preferred_element_type=f32
    )
    right_new = shampoo_beta * right_factor + (1.0 - shampoo_beta) * jnp.einsum(
        "nat,nab->ntb", own, tiles, preferred_element_type=f32
    )
    rotated = jnp.einsum("nab,nac->nbc", left_full, mixed, preferred_element_type=f32)
    first_new = first_beta * moment.reshape(blocks, B, width) + (1.0 - first_beta) * rotated
    second_new = (
        second_beta * second.reshape(blocks, B, width) + (1.0 - second_beta) * rotated * rotated
    )
    steps_full = normalized(first_new, second_new)
    for bit in range(nbits):
        other_steps = swapped(steps_full, "col", bit)
        lower = member >> bit & 1 == 0
        steps_full = join_pair(steps_full, other_steps, 2, lower)
    back = jnp.einsum("nab,ncb->nac", steps_full, right_basis, preferred_element_type=f32).astype(bf16)
    update = jnp.einsum("nab,nbc->nac", left_full, back, preferred_element_type=f32).astype(bf16)
    rows = blocks * B
    return (
        left_new,
        right_new,
        first_new.reshape(rows, width),
        second_new.reshape(rows, width),
        update.reshape(rows, width),
    )


def early_kernel(half_ref, g0_ref, g1_ref, h0_ref, h1_ref, right_own_ref, right_other_ref, x_ref, full_ref, gram_ref):
    tokens, width = g0_ref.shape
    at = pl.ds(pl.multiple_of(half_ref[0] * width, width), width)
    away = pl.ds(pl.multiple_of((1 - half_ref[0]) * width, width), width)

    @pl.when(pl.program_id(0) == 0)
    def _():
        full_ref[:tokens, at] = g0_ref[...]
        full_ref[tokens:, at] = g1_ref[...]
        full_ref[:tokens, away] = h0_ref[...]
        full_ref[tokens:, away] = h1_ref[...]
        gram_ref[...] = dot(full_ref[...], full_ref[...], 1, 1).astype(bf16)

    x = dot(full_ref[:, at], right_own_ref[0], 1, 0) + dot(full_ref[:, away], right_other_ref[0], 1, 0)
    x_ref[0] = x.astype(bf16)


def early(half, grads, right_own, right_other):
    blocks, width, order = right_own.shape
    tokens = 2 * grads[0].shape[0]
    whole = lambda n, s: (0, 0)
    column = pl.BlockSpec((1, width, width), lambda n, s: (n, 0, s[0]))
    return pl.pallas_call(
        early_kernel,
        grid_spec=pltpu.PrefetchScalarGridSpec(
            num_scalar_prefetch=1,
            grid=(blocks,),
            in_specs=[pl.BlockSpec((tokens // 2, width), whole)] * 4 + [column, column],
            out_specs=[
                pl.BlockSpec((1, tokens, width), lambda n, s: (n, 0, 0)),
                pl.BlockSpec((tokens, order), whole),
                pl.BlockSpec((tokens, tokens), whole),
            ],
        ),
        out_shape=[
            jax.ShapeDtypeStruct((blocks, tokens, width), bf16),
            jax.ShapeDtypeStruct((tokens, order), bf16),
            jax.ShapeDtypeStruct((tokens, tokens), bf16),
        ],
        compiler_params=pltpu.CompilerParams(vmem_limit_bytes=60 << 20),
        cost_estimate=pl.CostEstimate(
            flops=2 * blocks * tokens * order * width + 2 * tokens * tokens * order,
            bytes_accessed=2 * blocks * width * (order + tokens) + 4 * tokens * order,
            transcendentals=0,
        ),
        name="early",
    )(half, *grads, right_own, right_other)


def step_kernel(count, scal_ref, *refs):
    quads = refs[: 4 * count]
    (full_ref, gram_ref, x_ref, ql_own_ref, ql_other_ref, lf_ref, rf_ref, mo_ref, se_ref) = refs[
        4 * count : 4 * count + 9
    ]
    lo_ref, ro_ref, mout_ref, sout_ref, norm_ref, acts, left, right, mixed = refs[-9:]
    n, s = pl.program_id(0), pl.program_id(1)
    tokens, width = quads[0].shape
    half = scal_ref[0]
    at = pl.ds(pl.multiple_of(half * width, width), width)
    away = pl.ds(pl.multiple_of((1 - half) * width, width), width)

    for m in range(count):

        @pl.when((s == 0) & (n == m))
        def _():
            acts[:tokens, at] = quads[4 * m][...]
            acts[tokens:, at] = quads[4 * m + 1][...]
            acts[:tokens, away] = quads[4 * m + 2][...]
            acts[tokens:, away] = quads[4 * m + 3][...]

    @pl.when(s == 0)
    def _():
        a = acts[...]
        mixed[...] = dot(a, x_ref[0], 0, 0).astype(bf16)
        gram = dot(a, a, 1, 1).astype(bf16)
        left[...] = dot(acts[:, at], gram_ref[...], 0, 0).astype(bf16)
        right[...] = dot(full_ref[:, at], gram, 0, 0).astype(bf16)

    piece = mout_ref.shape[1]
    part = pl.ds(pl.multiple_of(s * piece, piece), piece)
    rot = dot(ql_own_ref[0], mixed[at, :], 0, 0) + dot(ql_other_ref[0], mixed[away, :], 0, 0)
    first_new = first_beta * mo_ref[0] + (1.0 - first_beta) * rot
    second_new = second_beta * se_ref[0] + (1.0 - second_beta) * rot * rot
    mout_ref[0] = first_new
    sout_ref[0] = second_new
    norm_ref[0] = normalized(first_new, second_new)
    lo_ref[0] = shampoo_beta * lf_ref[0] + (1.0 - shampoo_beta) * dot(left[...], acts[:, part], 1, 0)
    ro_ref[0] = shampoo_beta * rf_ref[0] + (1.0 - shampoo_beta) * dot(right[...], full_ref[:, part], 1, 0)


def step_blocks(scal, quads, shared, per_block, carried, pieces=2):
    count = len(quads)
    full, gram, x = shared
    lf, rf, mo, se = per_block[2:]
    tokens, order = full.shape
    _, width, _ = lf.shape
    piece = order // pieces
    factor = pl.BlockSpec((1, width, piece), lambda n, s, c: (c[1 + n], 0, s))
    moment = pl.BlockSpec((1, piece, width), lambda n, s, c: (c[1 + n], s, 0))
    once = lambda shape: pl.BlockSpec(shape, lambda n, s, c: (0, 0), pipeline_mode=pl.Buffered(1))
    in_specs = [once((tokens // 2, width))] * (4 * count) + [once((tokens, order)), once((tokens, tokens))]
    in_specs += [pl.BlockSpec((1, tokens, width), lambda n, s, c: (c[1 + n], 0, 0))]
    in_specs += [factor, factor, factor, factor, moment, moment]
    in_specs += [pl.BlockSpec(memory_space=pl.ANY)] * len(carried)
    first_carried = 1 + 4 * count + 9

    def kernel(*refs):
        at = first_carried
        step_kernel(count, *refs[:at], *refs[at + len(carried) :])

    shapes = [(lf.shape, f32), (rf.shape, f32), (mo.shape, f32), (se.shape, f32), ((count, order, width), bf16)]
    unit = 2 * tokens * tokens * width
    return pl.pallas_call(
        kernel,
        grid_spec=pltpu.PrefetchScalarGridSpec(
            num_scalar_prefetch=1,
            grid=(count, pieces),
            in_specs=in_specs,
            out_specs=[factor, factor, moment, moment, pl.BlockSpec((1, piece, width), lambda n, s, c: (n, s, 0))],
            scratch_shapes=[
                pltpu.VMEM((tokens, order), bf16),
                pltpu.VMEM((width, tokens), bf16),
                pltpu.VMEM((width, tokens), bf16),
                pltpu.VMEM((order, width), bf16),
            ],
        ),
        out_shape=[jax.ShapeDtypeStruct(*a) for a in shapes],
        input_output_aliases={first_carried + i: i for i in range(len(carried))},
        compiler_params=pltpu.CompilerParams(vmem_limit_bytes=60 << 20),
        cost_estimate=pl.CostEstimate(
            flops=14 * count * unit,
            bytes_accessed=count * 18 * order * width,
            transcendentals=2 * count * order * width,
        ),
        name="step",
    )(scal, *[a for q in quads for a in q], full, gram, x, *per_block, *carried)


def update_kernel(carried, scal_ref, n_own_ref, n_other_ref, q_own_ref, q_other_ref, ql_own_ref, ql_other_ref, *rest):
    out_ref, back = rest[carried:]
    width = q_own_ref.shape[1]
    half = scal_ref[0]
    b = dot(n_own_ref[0], q_own_ref[0], 1, 1) + dot(n_other_ref[0], q_other_ref[0], 1, 1)
    back[...] = b.astype(bf16)
    at = pl.ds(pl.multiple_of(half * width, width), width)
    away = pl.ds(pl.multiple_of((1 - half) * width, width), width)
    out_ref[0, at, :] = dot(ql_own_ref[0], back[...], 1, 0).astype(bf16)
    out_ref[0, away, :] = dot(ql_other_ref[0], back[...], 1, 0).astype(bf16)


def update_blocks(scal, norm_own, norm_other, right_own, ql_own, ql_other, carried):
    count, order, width = norm_own.shape
    blocks = ql_own.shape[0]
    stepped = pl.BlockSpec((1, order, width), lambda n, c: (n, 0, 0))
    basis = pl.BlockSpec((1, width, order), lambda n, c: (c[1 + n], 0, 0))
    unit = 2 * width * width * width
    return pl.pallas_call(
        functools.partial(update_kernel, len(carried)),
        grid_spec=pltpu.PrefetchScalarGridSpec(
            num_scalar_prefetch=1,
            grid=(count,),
            in_specs=[
                stepped,
                stepped,
                pl.BlockSpec((1, width, width), lambda n, c: (c[1 + n], 0, c[0])),
                pl.BlockSpec((1, width, width), lambda n, c: (c[1 + n], 0, 1 - c[0])),
                basis,
                basis,
            ]
            + [pl.BlockSpec(memory_space=pl.ANY)] * len(carried),
            out_specs=pl.BlockSpec((1, order, width), lambda n, c: (c[1 + n], 0, 0)),
            scratch_shapes=[pltpu.VMEM((order, width), bf16)],
        ),
        out_shape=jax.ShapeDtypeStruct((blocks, order, width), bf16),
        input_output_aliases={7: 0} if carried else {},
        compiler_params=pltpu.CompilerParams(vmem_limit_bytes=56 << 20),
        cost_estimate=pl.CostEstimate(
            flops=8 * count * unit, bytes_accessed=count * 8 * order * width, transcendentals=0
        ),
        name="update",
    )(scal, norm_own, norm_other, right_own, right_own, ql_own, ql_other, *carried)


def cube(acts, grad_out, left_factor, right_factor, left_basis, right_basis, moment, second):
    _, width = grad_out.shape
    blocks = left_factor.shape[0]
    size = lax.axis_size("col")
    col, y = lax.axis_index("col"), lax.axis_index("tok")
    half = col & 1
    high = col >> (size.bit_length() - 2) & 1
    first_block = (col >> 1 & (blocks - 1)) ^ jnp.where(high == y, 0, 2)

    def hop(array, mask):
        return lax.ppermute(array, "col", [(i, i ^ mask) for i in range(size)])

    def across(array):
        return lax.ppermute(array, "tok", [(0, 1), (1, 0)])

    core = lambda array: hop(array, 1)
    x_hop = lambda array: hop(array, 2)
    a_hop = lambda array: hop(array, 4)
    inner = high == y
    mirrored = hop(acts, size - 4)
    grads_away = across(grad_out)
    q_other = core(right_basis)
    ql_other = core(left_basis)
    grads = (grad_out, grads_away, core(grad_out), core(grads_away))
    near = jnp.where(inner, acts, mirrored)
    far = across(jnp.where(inner, mirrored, acts))
    near_x, near_a = x_hop(near), a_hop(near)
    far_x, far_a = x_hop(far), a_hop(far)
    near_d, far_d = x_hop(near_a), hop(far, 6)
    quad = lambda n, f: (n, f, core(n), core(f))
    quad0, quad_x, quad_a, quad_d = quad(near, far), quad(near_x, far_x), quad(near_a, far_a), quad(near_d, far_d)

    as_scal = lambda *v: jnp.stack([jnp.asarray(a, jnp.int32) for a in v])
    s0 = as_scal(half, first_block)
    s1 = as_scal(half, first_block ^ 1, first_block ^ 2, first_block ^ 3)
    x, full, gram = early(s0, grads, right_basis, q_other)
    shared = (full, gram, x)
    shaped = (blocks, B, width)
    states = (left_factor, right_factor, moment.reshape(shaped), second.reshape(shaped))
    per_block = (left_basis, ql_other, *states)
    *outs, norm0 = step_blocks(s0, [quad0], shared, per_block, [])
    *outs, norm1 = step_blocks(s1, [quad_x, quad_a, quad_d], shared, per_block, outs)
    away0, away1 = core(norm0), core(norm1)
    update = update_blocks(s0, norm0, away0, right_basis, left_basis, ql_other, [])
    update = update_blocks(s1, norm1, away1, right_basis, left_basis, ql_other, [update])
    rows = blocks * B
    left_new, right_new, first_new, second_new = outs
    return (
        left_new,
        right_new,
        first_new.reshape(rows, width),
        second_new.reshape(rows, width),
        update.reshape(rows, width),
    )


def shards(acts, grad_out, *rest):
    blocks = rest[0].shape[0]
    pairs = B // grad_out.shape[1] == 2 and lax.axis_size("tok") == 2
    if pairs and blocks == 4 and lax.axis_size("col") == 4 * blocks:
        return cube(acts, grad_out, *rest)
    return general(acts, grad_out, *rest)


def solution(mesh):
    in_specs = (
        P("tok", "col"),
        P("tok", "col"),
        P("tok", "col", None),
        P("tok", "col", None),
        P("tok", "col", None),
        P("tok", "col", None),
        P("tok", "col"),
        P("tok", "col"),
    )
    out_specs = (
        P("tok", "col", None),
        P("tok", "col", None),
        P("tok", "col"),
        P("tok", "col"),
        P("tok", "col"),
    )
    return jax.shard_map(shards, mesh=mesh, in_specs=in_specs, out_specs=out_specs, check_vma=False)
```

```python
import functools

import jax
import jax.numpy as jnp
from jax import lax
from jax.experimental import pallas as pl
from jax.experimental.pallas import tpu as pltpu
from jax.sharding import PartitionSpec as P

B = 1024


shampoo_beta = 0.95
first_beta = 0.9
second_beta = 0.95
first_corr = 1.0 - 0.9**4
second_corr = 1.0 - 0.95**4
epsilon = 1e-08

f32 = jnp.float32
bf16 = jnp.bfloat16


def dot(a, b, ca, cb):
    return lax.dot_general(a, b, (((ca,), (cb,)), ((), ())), preferred_element_type=f32)


def swapped(array, axis, distance):
    return lax.ppermute(array, axis, [(i, i ^ 1 << distance) for i in range(lax.axis_size(axis))])


def join_pair(current, incoming, axis, lower):
    width = current.shape[axis]
    shape = list(current.shape)
    shape[axis] = 2 * width
    joined = jnp.zeros(shape, current.dtype)
    mine_at = jnp.where(lower, 0, width)
    theirs_at = width - mine_at
    joined = lax.dynamic_update_slice_in_dim(joined, current, mine_at, axis)
    return lax.dynamic_update_slice_in_dim(joined, incoming, theirs_at, axis)


def normalized(first_new, second_new):
    return (first_new / first_corr / (jnp.sqrt(second_new / second_corr) + epsilon)).astype(bf16)


def general(acts, grad_out, left_factor, right_factor, left_basis, right_basis, moment, second):
    width = grad_out.shape[1]
    blocks = left_factor.shape[0]
    groups = B // width
    nbits = groups.bit_length() - 1
    member = lax.axis_index("col") % groups
    contract = (((0,), (0,)), ((), ()))
    whole = lax.all_gather(acts, "col", axis=1, tiled=True)
    block_rows = lax.all_to_all(whole, "tok", split_axis=1, concat_axis=0, tiled=True)
    all_grads = lax.all_gather(grad_out, "tok", axis=0, tiled=True)
    grad = lax.dot_general(block_rows, all_grads, contract, preferred_element_type=f32)
    own = grad.astype(bf16).reshape(blocks, B, width)
    tiles, left_full, right_full = (own, left_basis, right_basis)
    for bit in range(nbits):
        other = swapped((tiles, left_full, right_full), "col", bit)
        lower = member >> bit & 1 == 0
        tiles = join_pair(tiles, other[0], 2, lower)
        left_full = join_pair(left_full, other[1], 1, lower)
        right_full = join_pair(right_full, other[2], 1, lower)
    right_cols = lax.dynamic_slice_in_dim(right_full, member * width, width, 2)
    mixed = jnp.einsum("nab,nbc->nac", tiles, right_cols, preferred_element_type=f32).astype(bf16)
    lead = lax.dynamic_slice_in_dim(tiles, member * width, width, 1)
    left_new = shampoo_beta * left_factor + (1.0 - shampoo_beta) * jnp.einsum(
        "nab,ncb->nac", lead, tiles, preferred_element_type=f32
    )
    right_new = shampoo_beta * right_factor + (1.0 - shampoo_beta) * jnp.einsum(
        "nat,nab->ntb", own, tiles, preferred_element_type=f32
    )
    rotated = jnp.einsum("nab,nac->nbc", left_full, mixed, preferred_element_type=f32)
    first_new = first_beta * moment.reshape(blocks, B, width) + (1.0 - first_beta) * rotated
    second_new = (
        second_beta * second.reshape(blocks, B, width) + (1.0 - second_beta) * rotated * rotated
    )
    steps_full = normalized(first_new, second_new)
    for bit in range(nbits):
        other_steps = swapped(steps_full, "col", bit)
        lower = member >> bit & 1 == 0
        steps_full = join_pair(steps_full, other_steps, 2, lower)
    back = jnp.einsum("nab,ncb->nac", steps_full, right_basis, preferred_element_type=f32).astype(bf16)
    update = jnp.einsum("nab,nbc->nac", left_full, back, preferred_element_type=f32).astype(bf16)
    rows = blocks * B
    return (
        left_new,
        right_new,
        first_new.reshape(rows, width),
        second_new.reshape(rows, width),
        update.reshape(rows, width),
    )


def early_kernel(half_ref, g0_ref, g1_ref, h0_ref, h1_ref, right_own_ref, right_other_ref, x_ref, full_ref, gram_ref):
    tokens, width = g0_ref.shape
    at = pl.ds(pl.multiple_of(half_ref[0] * width, width), width)
    away = pl.ds(pl.multiple_of((1 - half_ref[0]) * width, width), width)

    @pl.when(pl.program_id(0) == 0)
    def _():
        full_ref[:tokens, at] = g0_ref[...]
        full_ref[tokens:, at] = g1_ref[...]
        full_ref[:tokens, away] = h0_ref[...]
        full_ref[tokens:, away] = h1_ref[...]
        gram_ref[...] = dot(full_ref[...], full_ref[...], 1, 1).astype(bf16)

    for j in range(x_ref.shape[0]):
        x = dot(full_ref[:, at], right_own_ref[j], 1, 0) + dot(full_ref[:, away], right_other_ref[j], 1, 0)
        x_ref[j] = x.astype(bf16)


def early(half, grads, right_own, right_other):
    blocks, width, order = right_own.shape
    tokens = 2 * grads[0].shape[0]
    whole = lambda n, s: (0, 0)
    many = 2
    column = pl.BlockSpec((many, width, width), lambda n, s: (n, 0, s[0]))
    return pl.pallas_call(
        early_kernel,
        grid_spec=pltpu.PrefetchScalarGridSpec(
            num_scalar_prefetch=1,
            grid=(blocks // many,),
            in_specs=[pl.BlockSpec((tokens // 2, width), whole)] * 4 + [column, column],
            out_specs=[
                pl.BlockSpec((many, tokens, width), lambda n, s: (n, 0, 0)),
                pl.BlockSpec((tokens, order), whole),
                pl.BlockSpec((tokens, tokens), whole),
            ],
        ),
        out_shape=[
            jax.ShapeDtypeStruct((blocks, tokens, width), bf16),
            jax.ShapeDtypeStruct((tokens, order), bf16),
            jax.ShapeDtypeStruct((tokens, tokens), bf16),
        ],
        compiler_params=pltpu.CompilerParams(vmem_limit_bytes=60 << 20),
        cost_estimate=pl.CostEstimate(
            flops=2 * blocks * tokens * order * width + 2 * tokens * tokens * order,
            bytes_accessed=2 * blocks * width * (order + tokens) + 4 * tokens * order,
            transcendentals=0,
        ),
        name="early",
    )(half, *grads, right_own, right_other)


def step_kernel(count, scal_ref, *refs):
    quads = refs[: 4 * count]
    (full_ref, gram_ref, x_ref, ql_own_ref, ql_other_ref, lf_ref, rf_ref, mo_ref, se_ref) = refs[
        4 * count : 4 * count + 9
    ]
    lo_ref, ro_ref, mout_ref, sout_ref, norm_ref, acts, left, right, mixed = refs[-9:]
    n, s = pl.program_id(0), pl.program_id(1)
    tokens, width = quads[0].shape
    half = scal_ref[0]
    at = pl.ds(pl.multiple_of(half * width, width), width)
    away = pl.ds(pl.multiple_of((1 - half) * width, width), width)

    for m in range(count):

        @pl.when((s == 0) & (n == m))
        def _():
            acts[:tokens, at] = quads[4 * m][...]
            acts[tokens:, at] = quads[4 * m + 1][...]
            acts[:tokens, away] = quads[4 * m + 2][...]
            acts[tokens:, away] = quads[4 * m + 3][...]

    @pl.when(s == 0)
    def _():
        a = acts[...]
        mixed[...] = dot(a, x_ref[0], 0, 0).astype(bf16)
        gram = dot(a, a, 1, 1).astype(bf16)
        left[...] = dot(acts[:, at], gram_ref[...], 0, 0).astype(bf16)
        right[...] = dot(full_ref[:, at], gram, 0, 0).astype(bf16)

    piece = mout_ref.shape[1]
    part = pl.ds(pl.multiple_of(s * piece, piece), piece)
    rot = dot(ql_own_ref[0], mixed[at, :], 0, 0) + dot(ql_other_ref[0], mixed[away, :], 0, 0)
    first_new = first_beta * mo_ref[0] + (1.0 - first_beta) * rot
    second_new = second_beta * se_ref[0] + (1.0 - second_beta) * rot * rot
    mout_ref[0] = first_new
    sout_ref[0] = second_new
    norm_ref[0] = normalized(first_new, second_new)
    lo_ref[0] = shampoo_beta * lf_ref[0] + (1.0 - shampoo_beta) * dot(left[...], acts[:, part], 1, 0)
    ro_ref[0] = shampoo_beta * rf_ref[0] + (1.0 - shampoo_beta) * dot(right[...], full_ref[:, part], 1, 0)


def step_blocks(scal, quads, shared, per_block, carried, pieces=2):
    count = len(quads)
    full, gram, x = shared
    lf, rf, mo, se = per_block[2:]
    tokens, order = full.shape
    _, width, _ = lf.shape
    piece = order // pieces
    factor = pl.BlockSpec((1, width, piece), lambda n, s, c: (c[1 + n], 0, s))
    moment = pl.BlockSpec((1, piece, width), lambda n, s, c: (c[1 + n], s, 0))
    once = lambda shape: pl.BlockSpec(shape, lambda n, s, c: (0, 0), pipeline_mode=pl.Buffered(1))
    in_specs = [once((tokens // 2, width))] * (4 * count) + [once((tokens, order)), once((tokens, tokens))]
    in_specs += [pl.BlockSpec((1, tokens, width), lambda n, s, c: (c[1 + n], 0, 0))]
    in_specs += [factor, factor, factor, factor, moment, moment]
    in_specs += [pl.BlockSpec(memory_space=pl.ANY)] * len(carried)
    first_carried = 1 + 4 * count + 9

    def kernel(*refs):
        at = first_carried
        step_kernel(count, *refs[:at], *refs[at + len(carried) :])

    shapes = [(lf.shape, f32), (rf.shape, f32), (mo.shape, f32), (se.shape, f32), ((count, order, width), bf16)]
    unit = 2 * tokens * tokens * width
    return pl.pallas_call(
        kernel,
        grid_spec=pltpu.PrefetchScalarGridSpec(
            num_scalar_prefetch=1,
            grid=(count, pieces),
            in_specs=in_specs,
            out_specs=[factor, factor, moment, moment, pl.BlockSpec((1, piece, width), lambda n, s, c: (n, s, 0))],
            scratch_shapes=[
                pltpu.VMEM((tokens, order), bf16),
                pltpu.VMEM((width, tokens), bf16),
                pltpu.VMEM((width, tokens), bf16),
                pltpu.VMEM((order, width), bf16),
            ],
        ),
        out_shape=[jax.ShapeDtypeStruct(*a) for a in shapes],
        input_output_aliases={first_carried + i: i for i in range(len(carried))},
        compiler_params=pltpu.CompilerParams(vmem_limit_bytes=60 << 20),
        cost_estimate=pl.CostEstimate(
            flops=14 * count * unit,
            bytes_accessed=count * 18 * order * width,
            transcendentals=2 * count * order * width,
        ),
        name="step",
    )(scal, *[a for q in quads for a in q], full, gram, x, *per_block, *carried)


def update_kernel(carried, scal_ref, n_own_ref, n_other_ref, q_own_ref, q_other_ref, ql_own_ref, ql_other_ref, *rest):
    out_ref, back = rest[carried:]
    width = q_own_ref.shape[1]
    half = scal_ref[0]
    b = dot(n_own_ref[0], q_own_ref[0], 1, 1) + dot(n_other_ref[0], q_other_ref[0], 1, 1)
    back[...] = b.astype(bf16)
    at = pl.ds(pl.multiple_of(half * width, width), width)
    away = pl.ds(pl.multiple_of((1 - half) * width, width), width)
    out_ref[0, at, :] = dot(ql_own_ref[0], back[...], 1, 0).astype(bf16)
    out_ref[0, away, :] = dot(ql_other_ref[0], back[...], 1, 0).astype(bf16)


def update_blocks(scal, norm_own, norm_other, right_own, ql_own, ql_other, carried):
    count, order, width = norm_own.shape
    blocks = ql_own.shape[0]
    stepped = pl.BlockSpec((1, order, width), lambda n, c: (n, 0, 0))
    basis = pl.BlockSpec((1, width, order), lambda n, c: (c[1 + n], 0, 0))
    unit = 2 * width * width * width
    return pl.pallas_call(
        functools.partial(update_kernel, len(carried)),
        grid_spec=pltpu.PrefetchScalarGridSpec(
            num_scalar_prefetch=1,
            grid=(count,),
            in_specs=[
                stepped,
                stepped,
                pl.BlockSpec((1, width, width), lambda n, c: (c[1 + n], 0, c[0])),
                pl.BlockSpec((1, width, width), lambda n, c: (c[1 + n], 0, 1 - c[0])),
                basis,
                basis,
            ]
            + [pl.BlockSpec(memory_space=pl.ANY)] * len(carried),
            out_specs=pl.BlockSpec((1, order, width), lambda n, c: (c[1 + n], 0, 0)),
            scratch_shapes=[pltpu.VMEM((order, width), bf16)],
        ),
        out_shape=jax.ShapeDtypeStruct((blocks, order, width), bf16),
        input_output_aliases={7: 0} if carried else {},
        compiler_params=pltpu.CompilerParams(vmem_limit_bytes=32 << 20),
        cost_estimate=pl.CostEstimate(
            flops=8 * count * unit, bytes_accessed=count * 8 * order * width, transcendentals=0
        ),
        name="update",
    )(scal, norm_own, norm_other, right_own, right_own, ql_own, ql_other, *carried)


def cube(acts, grad_out, left_factor, right_factor, left_basis, right_basis, moment, second):
    _, width = grad_out.shape
    blocks = left_factor.shape[0]
    size = lax.axis_size("col")
    col, y = lax.axis_index("col"), lax.axis_index("tok")
    half = col & 1
    high = col >> (size.bit_length() - 2) & 1
    first_block = (col >> 1 & (blocks - 1)) ^ jnp.where(high == y, 0, 2)

    def hop(array, mask):
        return lax.ppermute(array, "col", [(i, i ^ mask) for i in range(size)])

    def across(array):
        return lax.ppermute(array, "tok", [(0, 1), (1, 0)])

    core = lambda array: hop(array, 1)
    x_hop = lambda array: hop(array, 2)
    a_hop = lambda array: hop(array, 4)
    inner = high == y
    mirrored = hop(acts, size - 4)
    grads_away = across(grad_out)
    q_other = core(right_basis)
    ql_other = core(left_basis)
    grads = (grad_out, grads_away, core(grad_out), core(grads_away))
    near = jnp.where(inner, acts, mirrored)
    far = across(jnp.where(inner, mirrored, acts))
    near_x, near_a = x_hop(near), a_hop(near)
    far_x, far_a = x_hop(far), a_hop(far)
    near_d, far_d = x_hop(near_a), hop(far, 6)
    quad = lambda n, f: (n, f, core(n), core(f))
    quad0, quad_x, quad_a, quad_d = quad(near, far), quad(near_x, far_x), quad(near_a, far_a), quad(near_d, far_d)

    as_scal = lambda *v: jnp.stack([jnp.asarray(a, jnp.int32) for a in v])
    s0 = as_scal(half, first_block)
    s1 = as_scal(half, first_block ^ 1, first_block ^ 2, first_block ^ 3)
    x, full, gram = early(s0, grads, right_basis, q_other)
    shared = (full, gram, x)
    shaped = (blocks, B, width)
    states = (left_factor, right_factor, moment.reshape(shaped), second.reshape(shaped))
    per_block = (left_basis, ql_other, *states)
    *outs, norm0 = step_blocks(s0, [quad0], shared, per_block, [])
    *outs, norm1 = step_blocks(s1, [quad_x, quad_a, quad_d], shared, per_block, outs)
    away0, away1 = core(norm0), core(norm1)
    update = update_blocks(s0, norm0, away0, right_basis, left_basis, ql_other, [])
    update = update_blocks(s1, norm1, away1, right_basis, left_basis, ql_other, [update])
    rows = blocks * B
    left_new, right_new, first_new, second_new = outs
    return (
        left_new,
        right_new,
        first_new.reshape(rows, width),
        second_new.reshape(rows, width),
        update.reshape(rows, width),
    )


def shards(acts, grad_out, *rest):
    blocks = rest[0].shape[0]
    pairs = B // grad_out.shape[1] == 2 and lax.axis_size("tok") == 2
    if pairs and blocks == 4 and lax.axis_size("col") == 4 * blocks:
        return cube(acts, grad_out, *rest)
    return general(acts, grad_out, *rest)


def solution(mesh):
    in_specs = (
        P("tok", "col"),
        P("tok", "col"),
        P("tok", "col", None),
        P("tok", "col", None),
        P("tok", "col", None),
        P("tok", "col", None),
        P("tok", "col"),
        P("tok", "col"),
    )
    out_specs = (
        P("tok", "col", None),
        P("tok", "col", None),
        P("tok", "col"),
        P("tok", "col"),
        P("tok", "col"),
    )
    return jax.shard_map(shards, mesh=mesh, in_specs=in_specs, out_specs=out_specs, check_vma=False)
```
